128 devices in a mesh: ep: 8 (over x_lo, y), blk: 16 (over x_hi, z, core).
Axes of the slice: x: 4 (x_hi: 2, x_lo: 2; x = x_hi * 2 + x_lo), y: 4, z: 4, core: 2. Of those that a mesh axis runs over, the one named last changes fastest.
Arguments:
- tokens: bfloat16 [16384, 7168], P(('ep', 'blk')), may hold values from -6 to 6
- route: int32 [16384, 8], P(('ep', 'blk')), may hold values from 0 to 255, as said below
- gates: float32 [16384, 8], P(('ep', 'blk')), may hold values from 0.1 to 1
- cotangent: bfloat16 [16384, 7168], P(('ep', 'blk')), may hold values from -6 to 6
- w_gate: bfloat16 [8, 7168, 2048], P('ep', None, 'blk'), may hold values from -0.0625 to 0.0625
- w_up: bfloat16 [8, 7168, 2048], P('ep', None, 'blk'), may hold values from -0.0625 to 0.0625
- w_down: bfloat16 [8, 2048, 7168], P('ep', 'blk'), may hold values from -0.125 to 0.125
Outputs:
- mixed: bfloat16 [16384, 7168], P(('ep', 'blk'))
- grad_tokens: bfloat16 [16384, 7168], P(('ep', 'blk'))
- grad_gate: bfloat16 [8, 7168, 2048], P('ep', None, 'blk')
- grad_up: bfloat16 [8, 7168, 2048], P('ep', None, 'blk')
- grad_down: bfloat16 [8, 2048, 7168], P('ep', 'blk')
The draws below stay inside these ranges and needn't reach their ends.
Inputs may be any that keep to these rules, and one draw needn't show every extreme that they name: `route`: each row names 8 different experts; numbers below 8 are the window's experts. Among the 128 rows of one device each window expert is named by 1 to 4 rows, and in every draw one window expert is named by exactly 4 rows on every device.
All inputs are finite; a program needn't handle non-finite values.
Results may differ from the reference program's by a relative error of at most 0.025.
Values may be sent and summed in bfloat16 or wider, within the bound.
No kernel may reach another device: no remote copies, remote signals or barrier semaphores. Data moves between devices by JAX's collectives and lax.ppermute only.
A program may use at most 192 MiB of HBM per device.

```python
import math
import jax
import jax.numpy as jnp
from jax import lax

D = 7168
FF = 2048
TOP = 8
IDS = 256
TOK_DEV = 128
CAP = 4
EXPERTS = 8
TOKENS = 16384
N_BLK = 16


def draw_route(key, part):
    blocks = TOKENS // TOK_DEV
    key_count, key_full, key_rank, key_other, key_order = jax.random.split(key, 5)
    counts = jax.random.randint(key_count, (blocks, EXPERTS), 1, CAP + 1)
    fullest = jax.random.randint(key_full, (), 0, EXPERTS)
    counts = jnp.where(jnp.arange(EXPERTS)[None, :] == fullest, CAP, counts)
    raw_rank = jax.random.randint(key_rank, (blocks, EXPERTS, TOK_DEV), 0, 1 << 20)
    rank_scores = raw_rank * TOK_DEV + jnp.arange(TOK_DEV)
    sorted_order = jnp.argsort(rank_scores, axis=-1)
    ranks = jnp.argsort(sorted_order, axis=-1)
    member = jnp.transpose(ranks < counts[:, :, None], (0, 2, 1))
    member_all = jnp.pad(member, ((0, 0), (0, 0), (0, IDS - EXPERTS)))
    others = jax.random.randint(key_other, (blocks, TOK_DEV, IDS), 0, 1 << 20) * IDS + jnp.arange(IDS)
    inside = jnp.arange(IDS) < EXPERTS
    window_scores = jnp.where(member_all, (1 << 29) + jnp.arange(IDS), -1 - jnp.arange(IDS))
    scores = jnp.where(inside, window_scores, others)
    chosen_scores, chosen = lax.top_k(scores, TOP)
    shuffle = jax.random.randint(key_order, (blocks, TOK_DEV, TOP), 0, 1 << 20) * TOP + jnp.arange(TOP)
    shuffle_order = jnp.argsort(shuffle, axis=-1)
    ids = jnp.take_along_axis(chosen, shuffle_order, axis=-1)
    return ids.reshape(TOKENS, TOP).astype(jnp.int32)


def levels(own_key, shape, shards, low, largest):
    def one(axis_at, parts):
        draws = jax.random.uniform(jax.random.fold_in(jax.random.fold_in(own_key, 6), axis_at), (parts,), jnp.float32, low / len(shards), largest / len(shards))
        return jnp.repeat(jnp.exp(draws), shape[axis_at] // parts).reshape((-1,) + (1,) * (len(shape) - axis_at - 1))

    level = one(*shards[0])
    for cut in shards[1:]:
        level = level * one(*cut)
    return level


def normal_values(stream_key, dims, spread, limit, cuts=(), kind=jnp.bfloat16):
    values = jax.random.normal(stream_key, dims, jnp.float32) * spread
    if len(cuts) > 0:
        values = levels(stream_key, dims, cuts, -0.22, 0.18) * values
    return jnp.clip(values, min=-limit, max=limit).astype(kind)


def setup_inputs(seed: int = 0) -> dict:
    keys = jax.random.split(jax.random.key(seed), 8)
    return {
        "tokens": normal_values(keys[0], (TOKENS, D), 1.0, 6.0, ((0, 128),)),
        "route": draw_route(jax.random.fold_in(keys[7], 71), 0),
        "gates": jnp.clip(jnp.exp(math.log(1.0) - 2.3025851 * jax.random.uniform(keys[2], (TOKENS, TOP), jnp.float32) ** levels(keys[2], (TOKENS, TOP), ((0, 128),), -0.2, 0.2)), 0.1, 1.0),
        "cotangent": normal_values(keys[3], (TOKENS, D), 1.0, 6.0, ((0, 128),)),
        "w_gate": normal_values(keys[4], (EXPERTS, D, FF), D ** -0.5, 0.0625, ((0, 8), (2, 16))),
        "w_up": normal_values(keys[5], (EXPERTS, D, FF), D ** -0.5, 0.0625, ((0, 8), (2, 16))),
        "w_down": normal_values(keys[6], (EXPERTS, FF, D), FF ** -0.5, 0.125, ((0, 8), (1, 16))),
    }


def routing(route, gates):
    blocks = TOKENS // TOK_DEV
    ids = route.reshape(blocks, TOK_DEV, TOP)
    matches = ids[:, :, :, None] == jnp.arange(EXPERTS, dtype=jnp.int32)
    member = jnp.any(matches, axis=2)
    picks = gates.reshape(blocks, TOK_DEV, TOP)[:, :, :, None]
    weight = jnp.sum(jnp.where(matches, picks, jnp.zeros_like(picks)), axis=2)
    places = jnp.cumsum(member.astype(jnp.int32), axis=1) - 1
    picked = member[..., None] & (places[..., None] == jnp.arange(CAP, dtype=jnp.int32))
    return picked, weight


def expert_pass(operands):
    rows_x, rows_d, gate_w, up_w, down_w = operands
    count_rows = rows_x.shape[0]
    part = FF // N_BLK
    gate_pre = jnp.dot(rows_x, gate_w, preferred_element_type=jnp.float32)
    up_pre = jnp.dot(rows_x, up_w, preferred_element_type=jnp.float32)
    logistic = jax.nn.sigmoid(gate_pre)
    hidden = (gate_pre * logistic * up_pre).astype(jnp.bfloat16)
    hidden_blocks = hidden.reshape(count_rows, N_BLK, part).astype(jnp.float32)
    down_blocks = down_w.reshape(N_BLK, part, D).astype(jnp.float32)
    terms = jnp.einsum('rbf,bfd->brd', hidden_blocks, down_blocks)
    terms = lax.optimization_barrier(terms.astype(jnp.bfloat16)).astype(jnp.float32)
    expert_rows = jnp.sum(terms, axis=0).astype(jnp.bfloat16)
    hidden_grad = jnp.dot(rows_d, down_w.T, preferred_element_type=jnp.float32)
    grad_down = jnp.dot(hidden.T, rows_d, preferred_element_type=jnp.float32).astype(jnp.bfloat16)
    slope = logistic * (1.0 + gate_pre * (1.0 - logistic))
    gate_grad = (hidden_grad * up_pre * slope).astype(jnp.bfloat16)
    up_grad = (hidden_grad * gate_pre * logistic).astype(jnp.bfloat16)
    grad_gate = jnp.dot(rows_x.T, gate_grad, preferred_element_type=jnp.float32).astype(jnp.bfloat16)
    grad_up = jnp.dot(rows_x.T, up_grad, preferred_element_type=jnp.float32).astype(jnp.bfloat16)
    gate_blocks = gate_grad.reshape(count_rows, N_BLK, part).astype(jnp.float32)
    up_blocks = up_grad.reshape(count_rows, N_BLK, part).astype(jnp.float32)
    wg_blocks = gate_w.reshape(D, N_BLK, part).astype(jnp.float32)
    wu_blocks = up_w.reshape(D, N_BLK, part).astype(jnp.float32)
    back = jnp.einsum('rbf,dbf->brd', gate_blocks, wg_blocks) + jnp.einsum('rbf,dbf->brd', up_blocks, wu_blocks)
    back = lax.optimization_barrier(back.astype(jnp.bfloat16)).astype(jnp.float32)
    input_rows = jnp.sum(back, axis=0).astype(jnp.bfloat16)
    return expert_rows, input_rows, grad_gate, grad_up, grad_down


def reference(tokens, route, gates, cotangent, w_gate, w_up, w_down):
    blocks = TOKENS // TOK_DEV
    picked, weight = routing(route, gates)
    picked_f = picked.astype(jnp.float32)
    token_f = tokens.reshape(blocks, TOK_DEV, D).astype(jnp.float32)
    x_slots = jnp.einsum('btec,btd->ebcd', picked_f, token_f).astype(jnp.bfloat16)
    x_slots = x_slots.reshape(EXPERTS, blocks * CAP, D)
    slot_gate = jnp.einsum('btec,bte->ebc', picked_f, weight.astype(jnp.float32))
    cot_f = cotangent.reshape(blocks, TOK_DEV, D).astype(jnp.float32)
    d_slots = (jnp.einsum('btec,btd->ebcd', picked_f, cot_f) * slot_gate[..., None]).astype(jnp.bfloat16)
    d_slots = d_slots.reshape(EXPERTS, blocks * CAP, D)
    expert_rows, input_rows, grad_gate, grad_up, grad_down = lax.map(expert_pass, (x_slots, d_slots, w_gate, w_up, w_down))
    expert_rows = expert_rows.reshape(EXPERTS, blocks, CAP, D).astype(jnp.float32)
    input_rows = input_rows.reshape(EXPERTS, blocks, CAP, D).astype(jnp.float32)
    weighted = picked_f * weight.astype(jnp.float32)[..., None]
    mixed = jnp.einsum('btec,ebcd->btd', weighted, expert_rows, precision=lax.Precision.HIGHEST)
    mixed = mixed.reshape(TOKENS, D).astype(jnp.bfloat16)
    grad_tokens = jnp.einsum('btec,ebcd->btd', picked_f, input_rows, precision=lax.Precision.HIGHEST)
    grad_tokens = grad_tokens.reshape(TOKENS, D).astype(jnp.bfloat16)
    return (mixed, grad_tokens, grad_gate, grad_up, grad_down)
```

```python
import jax
import jax.numpy as jnp
from jax import lax
from jax.sharding import Mesh, PartitionSpec as P

CAP = 4
PAIR = ("xl", "y")
REST = ("xh", "z", "core")
PLANE = ("xl", "y", "xh")
SWAP = [(0, 1), (1, 0)]
F32 = jnp.float32
BF16 = jnp.bfloat16
def z_by(step):
    return [(i, (i + step) % 4) for i in range(4)]


def after(value, *first):
    return lax.optimization_barrier((value,) + first)[0]


def add(*terms):
    return sum(t.astype(F32) for t in terms).astype(BF16)


def near_z(rows):
    return lax.ppermute(rows, "z", z_by(1)), lax.ppermute(rows, "z", z_by(3))


def far_z(below, above):
    cut = below.shape[0] // 2
    return lax.ppermute(below[:cut], "z", z_by(1)), lax.ppermute(above[cut:], "z", z_by(3))


def scatter_z(parts, *first):
    cut = parts.shape[0] // 8
    part = [parts[i * cut : (i + 1) * cut] for i in range(8)]
    up_1 = lax.ppermute(after(parts[3 * cut : 5 * cut], *first), "z", z_by(1))
    down_1 = lax.ppermute(after(parts[5 * cut : 7 * cut], *first), "z", z_by(3))
    up_2 = lax.ppermute(add(part[2], up_1[cut:]), "z", z_by(1))
    down_2 = lax.ppermute(add(part[7], down_1[:cut]), "z", z_by(3))
    top = add(part[0], down_1[cut:], up_2)
    low = add(part[1], up_1[:cut], down_2)
    return jnp.concatenate([top, low], axis=0), (up_1, down_1)


def to_plane(slots):
    width = slots.shape[-1]
    twice = jnp.broadcast_to(slots.reshape(8, 1, CAP, width), (8, 2, CAP, width))
    moved = lax.all_to_all(
        twice.reshape(16, CAP, width), PLANE, split_axis=0, concat_axis=0, tiled=True
    )
    return moved.reshape(16 * CAP, width)


def to_slots(rows):
    width = rows.shape[1]
    sent = rows.reshape(16, CAP, width)
    back = lax.all_to_all(sent, PLANE, split_axis=0, concat_axis=0, tiled=True)
    return back.reshape(16 * CAP, width)


def local(tokens, route, gates, cotangent, w_gate, w_up, w_down):
    model_width = tokens.shape[1]
    half = w_down.shape[1]
    matches = route[:, :, None] == jnp.arange(8, dtype=jnp.int32)
    member = jnp.any(matches, axis=1)
    weight = jnp.sum(jnp.where(matches, gates[:, :, None], 0.0), axis=1)
    places = jnp.cumsum(member.astype(jnp.int32), axis=0) - 1
    picked = member[:, :, None] & (places[:, :, None] == jnp.arange(CAP, dtype=jnp.int32))
    picked_b = picked.astype(BF16).reshape(-1, 8 * CAP)
    picked_w = jnp.where(picked, weight[:, :, None], 0.0)
    twice_b = jnp.repeat(picked.astype(BF16), 2, axis=1).reshape(-1, 16 * CAP)
    twice_w = jnp.repeat(picked_w, 2, axis=1).reshape(-1, 16 * CAP)
    picked_w = picked_w.reshape(-1, 8 * CAP)
    slot_gate = jnp.sum(picked_w, axis=0)
    x_slots = jnp.einsum("ts,td->sd", picked_b, tokens, preferred_element_type=F32).astype(BF16)
    d_rows = jnp.einsum("ts,td->sd", picked_b, cotangent, preferred_element_type=F32)
    d_slots = (d_rows * slot_gate[:, None]).astype(BF16)

    gate_other = lax.ppermute(w_gate[0], "core", SWAP)
    up_other = lax.ppermute(w_up[0], "core", SWAP)
    down_other = lax.ppermute(w_down[0], "core", SWAP)

    plane_x = to_plane(x_slots)
    x_below, x_above = near_z(plane_x)
    plane_d = to_plane(after(d_slots, plane_x))
    parts = (w_gate[0], gate_other, w_up[0], up_other, w_down[0], down_other)
    parts = lax.optimization_barrier((plane_x,) + parts)[1:]
    w_in = jnp.concatenate(parts[:4], axis=1)
    w_out = jnp.concatenate(parts[4:], axis=0)
    w_in, w_out = lax.optimization_barrier((w_in, w_out))
    x_far = far_z(x_below, x_above)
    d_below, d_above = near_z(after(plane_d, x_below, x_above))
    rows_x = jnp.concatenate([plane_x, x_above, x_far[0], x_far[1], x_below], axis=0)

    pre = jnp.dot(rows_x, w_in, preferred_element_type=F32)
    gate_pre, up_pre = pre[:, : 2 * half], pre[:, 2 * half :]
    logistic = jax.nn.sigmoid(gate_pre)
    hidden = (gate_pre * logistic * up_pre).astype(BF16)
    hidden, gate_pre, up_pre = lax.optimization_barrier((hidden, gate_pre, up_pre))
    d_far = far_z(after(d_below, hidden), after(d_above, hidden))
    y_part = jnp.dot(hidden, w_out, preferred_element_type=F32).astype(BF16)
    y_rows, y_first = scatter_z(y_part, d_below, d_above)
    rows_d = jnp.concatenate([plane_d, d_above, d_far[0], d_far[1], d_below], axis=0)

    hidden_grad = jnp.einsum("rd,fd->rf", rows_d, w_out, preferred_element_type=F32)
    logistic = jax.nn.sigmoid(gate_pre)
    slope = logistic * (1.0 + gate_pre * (1.0 - logistic))
    gate_grad = (hidden_grad * up_pre * slope).astype(BF16)
    up_grad = (hidden_grad * gate_pre * logistic).astype(BF16)
    both = jnp.concatenate([gate_grad, up_grad], axis=1)
    q_part = jnp.einsum("rf,df->rd", both, w_in, preferred_element_type=F32).astype(BF16)
    q_rows, q_first = scatter_z(q_part, *y_first)

    both_own = jnp.concatenate([gate_grad[:, :half], up_grad[:, :half]], axis=1)
    both_other = jnp.concatenate([gate_grad[:, half:], up_grad[:, half:]], axis=1)
    in_other = jnp.einsum("rd,rf->df", rows_x, both_other, preferred_element_type=F32)
    out_other = jnp.einsum("rf,rd->fd", hidden[:, half:], rows_d, preferred_element_type=F32)
    in_got = lax.ppermute(in_other.astype(BF16), "core", SWAP)
    out_got = lax.ppermute(out_other.astype(BF16), "core", SWAP)
    in_own = jnp.einsum("rd,rf->df", rows_x, both_own, preferred_element_type=F32)
    out_own = jnp.einsum("rf,rd->fd", hidden[:, :half], rows_d, preferred_element_type=F32)
    grad_in = (in_own + in_got.astype(F32)).astype(BF16)
    grad_down = (out_own + out_got.astype(F32)).astype(BF16)

    back_out = to_slots(y_rows)
    back_in = to_slots(q_rows)
    mixed = jnp.dot(
        twice_w, back_out.astype(F32), precision=lax.Precision.HIGHEST
    ).astype(BF16)
    grad_tokens = jnp.dot(twice_b, back_in, preferred_element_type=F32).astype(BF16)
    return (mixed, grad_tokens, grad_in[None, :, :half], grad_in[None, :, half:], grad_down[None])


def solution(mesh):
    fine = Mesh(mesh.devices.reshape(2, 4, 2, 4, 2), PAIR + REST)
    rows = P(PAIR + REST, None)
    wide = P(PAIR, None, REST)
    tall = P(PAIR, REST, None)
    return jax.shard_map(
        local,
        mesh=fine,
        in_specs=(rows, rows, rows, rows, wide, wide, tall),
        out_specs=(rows, rows, wide, wide, tall),
        check_vma=False,
    )
```

```python
import jax
import jax.numpy as jnp
from jax import lax
from jax.sharding import Mesh, PartitionSpec as P

CAP = 4
LINE = 4 * CAP
PAIR = ("xl", "y")
REST = ("xh", "z", "core")
PLANE = ("xl", "xh", "y")
SWAP = [(0, 1), (1, 0)]
F32 = jnp.float32
BF16 = jnp.bfloat16
def z_by(step):
    return [(i, (i + step) % 4) for i in range(4)]


def tie(*values):
    return lax.optimization_barrier(values)


def add(*terms):
    return sum(t.astype(F32) for t in terms).astype(BF16)


def near_z(rows):
    return lax.ppermute(rows, "z", z_by(1)), lax.ppermute(rows, "z", z_by(3))


def halves(below, above):
    cut = below.shape[0] // 2
    return below[:cut], above[cut:]


def far_z(low, high):
    return lax.ppermute(low, "z", z_by(1)), lax.ppermute(high, "z", z_by(3))


def across(rows):
    return lax.ppermute(rows, "xh", SWAP)


def near_x(below, above):
    return across(jnp.concatenate([below[:LINE], above[:LINE]], axis=0))


def all_rows(plane, below, above, low, high, near, far):
    return jnp.concatenate(
        [plane, above, near[LINE:], low, high, far, below, near[:LINE]], axis=0
    )


def scatter_in(parts):
    cut = parts.shape[0] // 8
    return parts[3 * cut : 5 * cut], parts[5 * cut : 7 * cut]


def scatter_far(parts, up_1, down_1):
    cut = parts.shape[0] // 8
    return add(parts[2 * cut : 3 * cut], up_1[cut:]), add(parts[7 * cut :], down_1[:cut])


def scatter_out(parts, up_1, down_1, up_2, down_2):
    cut = parts.shape[0] // 8
    top = add(parts[:cut], down_1[cut:], up_2)
    low = add(parts[cut : 2 * cut], up_1[:cut], down_2)
    return jnp.concatenate([top, low], axis=0)


def relative(blocks):
    xl, xh = lax.axis_index("xl"), lax.axis_index("xh")
    same = jnp.where(xl == 0, blocks[:2], blocks[2:])
    other = jnp.where(xl == 0, blocks[2:], blocks[:2])
    own = jnp.where(xh == 0, same[0], same[1])
    far = jnp.where(xh == 0, same[1], same[0])
    return jnp.concatenate([own, other.reshape(2 * LINE, -1), far], axis=0)


def absolute(rows):
    xl, xh = lax.axis_index("xl"), lax.axis_index("xh")
    own, far = rows[:LINE], rows[3 * LINE :]
    other = rows[LINE : 3 * LINE]
    same = jnp.concatenate([jnp.where(xh == 0, own, far), jnp.where(xh == 0, far, own)], axis=0)
    first, second = jnp.where(xl == 0, same, other), jnp.where(xl == 0, other, same)
    return jnp.concatenate([first, second], axis=0)


def to_plane(slots):
    width = slots.shape[-1]
    twice = jnp.broadcast_to(slots.reshape(2, 1, 4, CAP, width), (2, 2, 4, CAP, width))
    return twice.reshape(16, CAP, width)


def move_plane(twice):
    moved = lax.all_to_all(twice, PLANE, split_axis=0, concat_axis=0, tiled=True)
    return relative(moved.reshape(4, LINE, -1))


def to_slots(rows):
    width = rows.shape[1]
    sent = absolute(rows).reshape(16, CAP, width)
    back = lax.all_to_all(sent, PLANE, split_axis=0, concat_axis=0, tiled=True)
    return back.reshape(16 * CAP, width)


def local(tokens, route, gates, cotangent, w_gate, w_up, w_down):
    model_width = tokens.shape[1]
    half = w_down.shape[1]
    matches = route[:, :, None] == jnp.arange(8, dtype=jnp.int32)
    member = jnp.any(matches, axis=1)
    weight = jnp.sum(jnp.where(matches, gates[:, :, None], 0.0), axis=1)
    rows = jnp.arange(route.shape[0])
    earlier = (rows[None, :] < rows[:, None]).astype(BF16)
    places = jnp.dot(earlier, member.astype(BF16), preferred_element_type=F32)
    picked = member[:, :, None] & (places[:, :, None] == jnp.arange(CAP, dtype=F32))
    picked_b = picked.astype(BF16).reshape(-1, 8 * CAP)
    picked_w = jnp.where(picked, weight[:, :, None], 0.0)
    pair = lambda a: jnp.broadcast_to(a.reshape(-1, 2, 1, 4, CAP), (a.shape[0], 2, 2, 4, CAP))
    twice_b = pair(picked.astype(BF16)).reshape(-1, 16 * CAP)
    twice_w = pair(picked_w).reshape(-1, 16 * CAP)
    picked_w = picked_w.reshape(-1, 8 * CAP)
    slot_gate = jnp.sum(picked_w, axis=0)
    x_slots = jnp.einsum("ts,td->sd", picked_b, tokens, preferred_element_type=F32).astype(BF16)
    gate_other = lax.ppermute(w_gate[0], "core", SWAP)
    up_other = lax.ppermute(w_up[0], "core", SWAP)
    down_other = lax.ppermute(w_down[0], "core", SWAP)

    d_rows = jnp.einsum("ts,td->sd", picked_b, cotangent, preferred_element_type=F32)
    d_slots = (d_rows * slot_gate[:, None]).astype(BF16)
    plane_x = move_plane(to_plane(x_slots))
    x_near = near_z(plane_x[: 3 * LINE])
    d_twice, plane_x = tie(to_plane(d_slots), plane_x)
    plane_d = move_plane(d_twice)
    x_far = far_z(*tie(*halves(*x_near)))
    x_side = near_x(*x_near)
    d_ring, *x_near = tie(plane_d[: 3 * LINE], *x_near)
    d_near = near_z(d_ring)
    x_last = across(x_far[0][:LINE])
    tied = tie(w_gate[0], gate_other, w_up[0], up_other, w_down[0], down_other, *x_far)
    parts, x_far = tied[:6], tied[6:]
    w_in = jnp.concatenate(parts[:4], axis=1)
    w_out = jnp.concatenate(parts[4:], axis=0)
    w_in, w_out = tie(w_in, w_out)
    rows_x = all_rows(plane_x, *x_near, *x_far, x_side, x_last)

    pre = jnp.dot(rows_x, w_in, preferred_element_type=F32)
    gate_pre, up_pre = pre[:, : 2 * half], pre[:, 2 * half :]
    logistic = jax.nn.sigmoid(gate_pre)
    hidden = (gate_pre * logistic * up_pre).astype(BF16)
    hidden, gate_pre, up_pre = tie(hidden, gate_pre, up_pre)
    d_low, d_high = tie(*halves(*d_near))
    d_far = far_z(d_low, d_high)
    d_side = near_x(*d_near)
    y_part = jnp.dot(hidden, w_out, preferred_element_type=F32).astype(BF16)
    d_last = across(d_far[0][:LINE])
    y_up, y_down, *d_far = tie(*scatter_in(y_part), *d_far)
    y_1 = far_z(y_up, y_down)
    rows_d = all_rows(plane_d, *d_near, *d_far, d_side, d_last)

    hidden_grad = jnp.einsum("rd,fd->rf", rows_d, w_out, preferred_element_type=F32)
    logistic = jax.nn.sigmoid(gate_pre)
    slope = logistic * (1.0 + gate_pre * (1.0 - logistic))
    gate_grad = (hidden_grad * up_pre * slope).astype(BF16)
    up_grad = (hidden_grad * gate_pre * logistic).astype(BF16)
    both = jnp.concatenate([gate_grad, up_grad], axis=1)
    q_part = jnp.einsum("rf,df->rd", both, w_in, preferred_element_type=F32).astype(BF16)
    y_up, y_down, *y_1 = tie(*scatter_far(y_part, *y_1), *y_1)
    y_2 = far_z(y_up, y_down)
    q_up, q_down, *y_1 = tie(*scatter_in(q_part), *y_1)
    q_1 = far_z(q_up, q_down)
    y_rows = scatter_out(y_part, *y_1, *y_2)
    back_out = to_slots(y_rows)
    q_up, q_down, back_out, *q_1 = tie(*scatter_far(q_part, *q_1), back_out, *q_1)
    q_2 = far_z(q_up, q_down)
    q_rows = scatter_out(q_part, *q_1, *q_2)

    gate_grad, up_grad, hidden, q_part = tie(gate_grad, up_grad, hidden, q_part)
    late = lambda a, b: jnp.einsum("rd,rf->df", a, b, preferred_element_type=F32)
    gate_got = lax.ppermute(late(rows_x, gate_grad[:, half:]).astype(BF16), "core", SWAP)
    up_got = lax.ppermute(late(rows_x, up_grad[:, half:]).astype(BF16), "core", SWAP)
    out_got = lax.ppermute(late(hidden[:, half:], rows_d).astype(BF16), "core", SWAP)
    grad_gate = add(late(rows_x, gate_grad[:, :half]), gate_got)
    grad_up = add(late(rows_x, up_grad[:, :half]), up_got)
    grad_down = add(late(hidden[:, :half], rows_d), out_got)

    back_in = to_slots(q_rows)
    mixed = jnp.dot(
        twice_w, back_out.astype(F32), precision=lax.Precision.HIGHEST
    ).astype(BF16)
    grad_tokens = jnp.dot(twice_b, back_in, preferred_element_type=F32).astype(BF16)
    return (mixed, grad_tokens, grad_gate[None], grad_up[None], grad_down[None])


def solution(mesh):
    fine = Mesh(mesh.devices.reshape(2, 4, 2, 4, 2), PAIR + REST)
    rows = P(PAIR + REST, None)
    wide = P(PAIR, None, REST)
    tall = P(PAIR, REST, None)
    return jax.shard_map(
        local,
        mesh=fine,
        in_specs=(rows, rows, rows, rows, wide, wide, tall),
        out_specs=(rows, rows, wide, wide, tall),
        check_vma=False,
    )
```

```python
import jax
import jax.numpy as jnp
from jax import lax
from jax.sharding import Mesh, PartitionSpec as P

CAP = 4
LINE = 4 * CAP
PAIR = ("xl", "y")
REST = ("xh", "z", "core")
PLANE = ("xl", "xh", "y")
SWAP = [(0, 1), (1, 0)]
F32 = jnp.float32
BF16 = jnp.bfloat16
def z_by(step):
    return [(i, (i + step) % 4) for i in range(4)]


def tie(*values):
    return lax.optimization_barrier(values)


def add(*terms):
    return sum(t.astype(F32) for t in terms).astype(BF16)


def near_z(rows):
    return lax.ppermute(rows, "z", z_by(1)), lax.ppermute(rows, "z", z_by(3))


def halves(below, above):
    cut = below.shape[0] // 2
    return below[:cut], above[cut:]


def far_z(low, high):
    return lax.ppermute(low, "z", z_by(1)), lax.ppermute(high, "z", z_by(3))


def across(rows):
    return lax.ppermute(rows, "xh", SWAP)


def near_x(below, above):
    return across(jnp.concatenate([below[:LINE], above[:LINE]], axis=0))


def all_rows(plane, below, above, low, high, near, far):
    return jnp.concatenate(
        [plane, above, near[LINE:], low, high, far, below, near[:LINE]], axis=0
    )


def scatter_in(parts):
    cut = parts.shape[0] // 8
    return parts[3 * cut : 5 * cut], parts[5 * cut : 7 * cut]


def scatter_far(parts, up_1, down_1):
    cut = parts.shape[0] // 8
    return add(parts[2 * cut : 3 * cut], up_1[cut:]), add(parts[7 * cut :], down_1[:cut])


def scatter_out(parts, up_1, down_1, up_2, down_2):
    cut = parts.shape[0] // 8
    top = add(parts[:cut], down_1[cut:], up_2)
    low = add(parts[cut : 2 * cut], up_1[:cut], down_2)
    return jnp.concatenate([top, low], axis=0)


def relative(blocks):
    xl, xh = lax.axis_index("xl"), lax.axis_index("xh")
    same = jnp.where(xl == 0, blocks[:2], blocks[2:])
    other = jnp.where(xl == 0, blocks[2:], blocks[:2])
    own = jnp.where(xh == 0, same[0], same[1])
    far = jnp.where(xh == 0, same[1], same[0])
    return jnp.concatenate([own, other.reshape(2 * LINE, -1), far], axis=0)


def absolute(rows):
    xl, xh = lax.axis_index("xl"), lax.axis_index("xh")
    own, far = rows[:LINE], rows[3 * LINE :]
    other = rows[LINE : 3 * LINE]
    same = jnp.concatenate([jnp.where(xh == 0, own, far), jnp.where(xh == 0, far, own)], axis=0)
    first, second = jnp.where(xl == 0, same, other), jnp.where(xl == 0, other, same)
    return jnp.concatenate([first, second], axis=0)


def to_plane(slots):
    width = slots.shape[-1]
    twice = jnp.broadcast_to(slots.reshape(2, 1, 4, CAP, width), (2, 2, 4, CAP, width))
    return twice.reshape(16, CAP, width)


def move_plane(twice):
    moved = lax.all_to_all(twice, PLANE, split_axis=0, concat_axis=0, tiled=True)
    return relative(moved.reshape(4, LINE, -1))


def to_slots(rows):
    width = rows.shape[1]
    sent = absolute(rows).reshape(16, CAP, width)
    back = lax.all_to_all(sent, PLANE, split_axis=0, concat_axis=0, tiled=True)
    return back.reshape(16 * CAP, width)


def local(tokens, route, gates, cotangent, w_gate, w_up, w_down):
    model_width = tokens.shape[1]
    half = w_down.shape[1]
    matches = route[:, :, None] == jnp.arange(8, dtype=jnp.int32)
    member = jnp.any(matches, axis=1)
    weight = jnp.sum(jnp.where(matches, gates[:, :, None], 0.0), axis=1)
    rows = jnp.arange(route.shape[0])
    earlier = (rows[None, :] < rows[:, None]).astype(BF16)
    places = jnp.dot(earlier, member.astype(BF16), preferred_element_type=F32)
    picked = member[:, :, None] & (places[:, :, None] == jnp.arange(CAP, dtype=F32))
    picked_b = picked.astype(BF16).reshape(-1, 8 * CAP)
    picked_w = jnp.where(picked, weight[:, :, None], 0.0)
    pair = lambda a: jnp.broadcast_to(a.reshape(-1, 2, 1, 4, CAP), (a.shape[0], 2, 2, 4, CAP))
    twice_b = pair(picked.astype(BF16)).reshape(-1, 16 * CAP)
    twice_w = pair(picked_w).reshape(-1, 16 * CAP)
    picked_w = picked_w.reshape(-1, 8 * CAP)
    slot_gate = jnp.sum(picked_w, axis=0)
    x_slots = jnp.einsum("ts,td->sd", picked_b, tokens, preferred_element_type=F32).astype(BF16)
    gate_other = lax.ppermute(w_gate[0], "core", SWAP)
    up_other = lax.ppermute(w_up[0], "core", SWAP)
    down_other = lax.ppermute(w_down[0], "core", SWAP)

    d_rows = jnp.einsum("ts,td->sd", picked_b, cotangent, preferred_element_type=F32)
    d_slots = (d_rows * slot_gate[:, None]).astype(BF16)
    plane_x = move_plane(to_plane(x_slots))
    x_near = near_z(plane_x[: 3 * LINE])
    d_twice, plane_x = tie(to_plane(d_slots), plane_x)
    plane_d = move_plane(d_twice)
    x_far = far_z(*tie(*halves(*x_near)))
    x_side = near_x(*x_near)
    d_ring, *x_near = tie(plane_d[: 3 * LINE], *x_near)
    d_near = near_z(d_ring)
    x_last = across(x_far[0][:LINE])
    tied = tie(w_gate[0], gate_other, w_up[0], up_other, w_down[0], down_other, *x_far)
    parts, x_far = tied[:6], tied[6:]
    w_in = jnp.concatenate(parts[:4], axis=1)
    w_out = jnp.concatenate(parts[4:], axis=0)
    w_in, w_out = tie(w_in, w_out)
    rows_x = all_rows(plane_x, *x_near, *x_far, x_side, x_last)

    pre = jnp.dot(rows_x, w_in, preferred_element_type=F32)
    gate_pre, up_pre = pre[:, : 2 * half], pre[:, 2 * half :]
    logistic = jax.nn.sigmoid(gate_pre)
    hidden = (gate_pre * logistic * up_pre).astype(BF16)
    hidden, gate_pre, up_pre = tie(hidden, gate_pre, up_pre)
    d_low, d_high = tie(*halves(*d_near))
    d_far = far_z(d_low, d_high)
    d_side = near_x(*d_near)
    y_part = jnp.dot(hidden, w_out, preferred_element_type=F32).astype(BF16)
    d_last = across(d_far[0][:LINE])
    y_up, y_down, *d_far = tie(*scatter_in(y_part), *d_far)
    y_1 = far_z(y_up, y_down)
    rows_d = all_rows(plane_d, *d_near, *d_far, d_side, d_last)

    hidden_grad = jnp.einsum("rd,fd->rf", rows_d, w_out, preferred_element_type=F32)
    logistic = jax.nn.sigmoid(gate_pre)
    slope = logistic * (1.0 + gate_pre * (1.0 - logistic))
    gate_grad = (hidden_grad * up_pre * slope).astype(BF16)
    up_grad = (hidden_grad * gate_pre * logistic).astype(BF16)
    late = lambda a, b: jnp.einsum("rd,rf->df", a, b, preferred_element_type=F32)
    gate_part = late(rows_x, gate_grad[:, half:]).astype(BF16)
    up_part = late(rows_x, up_grad[:, half:]).astype(BF16)
    out_part = late(hidden[:, half:], rows_d).astype(BF16)
    gate_grad, up_grad, gate_part, up_part, out_part = tie(
        gate_grad, up_grad, gate_part, up_part, out_part
    )
    both = jnp.concatenate([gate_grad, up_grad], axis=1)
    q_part = jnp.einsum("rf,df->rd", both, w_in, preferred_element_type=F32).astype(BF16)
    y_up, y_down, *y_1 = tie(*scatter_far(y_part, *y_1), *y_1)
    y_2 = far_z(y_up, y_down)
    q_up, q_down, *y_1 = tie(*scatter_in(q_part), *y_1)
    q_1 = far_z(q_up, q_down)
    y_rows = scatter_out(y_part, *y_1, *y_2)
    back_out = to_slots(y_rows)
    q_up, q_down, back_out, *q_1 = tie(*scatter_far(q_part, *q_1), back_out, *q_1)
    q_2 = far_z(q_up, q_down)
    q_rows = scatter_out(q_part, *q_1, *q_2)

    gate_got = lax.ppermute(gate_part, "core", SWAP)
    up_got = lax.ppermute(up_part, "core", SWAP)
    out_got = lax.ppermute(out_part, "core", SWAP)
    grad_gate = add(late(rows_x, gate_grad[:, :half]), gate_got)
    grad_up = add(late(rows_x, up_grad[:, :half]), up_got)
    grad_down = add(late(hidden[:, :half], rows_d), out_got)

    back_in = to_slots(q_rows)
    mixed = jnp.dot(
        twice_w, back_out.astype(F32), precision=lax.Precision.HIGHEST
    ).astype(BF16)
    grad_tokens = jnp.dot(twice_b, back_in, preferred_element_type=F32).astype(BF16)
    return (mixed, grad_tokens, grad_gate[None], grad_up[None], grad_down[None])


def solution(mesh):
    fine = Mesh(mesh.devices.reshape(2, 4, 2, 4, 2), PAIR + REST)
    rows = P(PAIR + REST, None)
    wide = P(PAIR, None, REST)
    tall = P(PAIR, REST, None)
    return jax.shard_map(
        local,
        mesh=fine,
        in_specs=(rows, rows, rows, rows, wide, wide, tall),
        out_specs=(rows, rows, wide, wide, tall),
        check_vma=False,
    )
```

```python
import jax
import jax.numpy as jnp
from jax import lax
from jax.sharding import Mesh, PartitionSpec as P

CAP = 4
LINE = 4 * CAP
PAIR = ("xl", "y")
REST = ("xh", "z", "core")
PLANE = ("xl", "xh", "y")
SWAP = [(0, 1), (1, 0)]
F32 = jnp.float32
BF16 = jnp.bfloat16
def z_by(step):
    return [(i, (i + step) % 4) for i in range(4)]


def tie(*values):
    return lax.optimization_barrier(values)


def add(*terms):
    return sum(t.astype(F32) for t in terms).astype(BF16)


def near_z(rows):
    return lax.ppermute(rows, "z", z_by(1)), lax.ppermute(rows, "z", z_by(3))


def halves(below, above):
    cut = below.shape[0] // 2
    return below[:cut], above[cut:]


def far_z(low, high):
    return lax.ppermute(low, "z", z_by(1)), lax.ppermute(high, "z", z_by(3))


def across(rows):
    return lax.ppermute(rows, "xh", SWAP)


def near_x(below, above):
    return across(jnp.concatenate([below[:LINE], above[:LINE]], axis=0))


def all_rows(plane, below, above, low, high, near, far):
    return jnp.concatenate(
        [plane, above, near[LINE:], low, high, far, below, near[:LINE]], axis=0
    )


def scatter_in(parts):
    cut = parts.shape[0] // 8
    return parts[3 * cut : 5 * cut], parts[5 * cut : 7 * cut]


def scatter_far(parts, up_1, down_1):
    cut = parts.shape[0] // 8
    return add(parts[2 * cut : 3 * cut], up_1[cut:]), add(parts[7 * cut :], down_1[:cut])


def scatter_out(parts, up_1, down_1, up_2, down_2):
    cut = parts.shape[0] // 8
    top = add(parts[:cut], down_1[cut:], up_2)
    low = add(parts[cut : 2 * cut], up_1[:cut], down_2)
    return jnp.concatenate([top, low], axis=0)


def relative(blocks):
    xl, xh = lax.axis_index("xl"), lax.axis_index("xh")
    same = jnp.where(xl == 0, blocks[:2], blocks[2:])
    other = jnp.where(xl == 0, blocks[2:], blocks[:2])
    own = jnp.where(xh == 0, same[0], same[1])
    far = jnp.where(xh == 0, same[1], same[0])
    return jnp.concatenate([own, other.reshape(2 * LINE, -1), far], axis=0)


def absolute(rows):
    xl, xh = lax.axis_index("xl"), lax.axis_index("xh")
    own, far = rows[:LINE], rows[3 * LINE :]
    other = rows[LINE : 3 * LINE]
    same = jnp.concatenate([jnp.where(xh == 0, own, far), jnp.where(xh == 0, far, own)], axis=0)
    first, second = jnp.where(xl == 0, same, other), jnp.where(xl == 0, other, same)
    return jnp.concatenate([first, second], axis=0)


def to_plane(slots):
    width = slots.shape[-1]
    twice = jnp.broadcast_to(slots.reshape(2, 1, 4, CAP, width), (2, 2, 4, CAP, width))
    return twice.reshape(16, CAP, width)


def move_plane(twice):
    moved = lax.all_to_all(twice, PLANE, split_axis=0, concat_axis=0, tiled=True)
    return relative(moved.reshape(4, LINE, -1))


def to_slots(rows):
    width = rows.shape[1]
    sent = absolute(rows).reshape(16, CAP, width)
    back = lax.all_to_all(sent, PLANE, split_axis=0, concat_axis=0, tiled=True)
    return back


def local(tokens, route, gates, cotangent, w_gate, w_up, w_down):
    model_width = tokens.shape[1]
    half = w_down.shape[1]
    matches = route[:, :, None] == jnp.arange(8, dtype=jnp.int32)
    member = jnp.any(matches, axis=1)
    weight = jnp.sum(jnp.where(matches, gates[:, :, None], 0.0), axis=1)
    rows = jnp.arange(route.shape[0])
    earlier = (rows[None, :] < rows[:, None]).astype(BF16)
    places = jnp.dot(earlier, member.astype(BF16), preferred_element_type=F32)
    picked = member[:, :, None] & (places[:, :, None] == jnp.arange(CAP, dtype=F32))
    picked_b = picked.astype(BF16).reshape(-1, 8 * CAP)
    picked_w = jnp.where(picked, weight[:, :, None], 0.0)
    pair = lambda a: jnp.broadcast_to(a.reshape(-1, 2, 1, 4, CAP), (a.shape[0], 2, 2, 4, CAP))
    twice_b = pair(picked.astype(BF16)).reshape(-1, 16, CAP)
    twice_w = pair(picked_w).reshape(-1, 16, CAP)
    picked_w = picked_w.reshape(-1, 8 * CAP)
    slot_gate = jnp.sum(picked_w, axis=0)
    x_slots = jnp.einsum("ts,td->sd", picked_b, tokens, preferred_element_type=F32).astype(BF16)
    gate_other = lax.ppermute(w_gate[0], "core", SWAP)
    up_other = lax.ppermute(w_up[0], "core", SWAP)
    down_other = lax.ppermute(w_down[0], "core", SWAP)

    d_rows = jnp.einsum("ts,td->sd", picked_b, cotangent, preferred_element_type=F32)
    d_slots = (d_rows * slot_gate[:, None]).astype(BF16)
    plane_x = move_plane(to_plane(x_slots))
    x_near = near_z(plane_x[: 3 * LINE])
    d_twice, plane_x = tie(to_plane(d_slots), plane_x)
    plane_d = move_plane(d_twice)
    x_far = far_z(*tie(*halves(*x_near)))
    x_side = near_x(*x_near)
    d_ring, *x_near = tie(plane_d[: 3 * LINE], *x_near)
    d_near = near_z(d_ring)
    x_last = across(x_far[0][:LINE])
    tied = tie(w_gate[0], gate_other, w_up[0], up_other, w_down[0], down_other, *x_far)
    parts, x_far = tied[:6], tied[6:]
    w_in = jnp.concatenate(parts[:4], axis=1)
    w_out = jnp.concatenate(parts[4:], axis=0)
    w_in, w_out = tie(w_in, w_out)
    rows_x = all_rows(plane_x, *x_near, *x_far, x_side, x_last)

    pre = jnp.dot(rows_x, w_in, preferred_element_type=F32)
    gate_pre, up_pre = pre[:, : 2 * half], pre[:, 2 * half :]
    logistic = jax.nn.sigmoid(gate_pre)
    hidden = (gate_pre * logistic * up_pre).astype(BF16)
    hidden, gate_pre, up_pre = tie(hidden, gate_pre, up_pre)
    d_low, d_high = tie(*halves(*d_near))
    d_far = far_z(d_low, d_high)
    d_side = near_x(*d_near)
    y_part = jnp.dot(hidden, w_out, preferred_element_type=F32).astype(BF16)
    d_last = across(d_far[0][:LINE])
    y_up, y_down, *d_far = tie(*scatter_in(y_part), *d_far)
    y_1 = far_z(y_up, y_down)
    rows_d = all_rows(plane_d, *d_near, *d_far, d_side, d_last)

    hidden_grad = jnp.einsum("rd,fd->rf", rows_d, w_out, preferred_element_type=F32)
    logistic = jax.nn.sigmoid(gate_pre)
    slope = logistic * (1.0 + gate_pre * (1.0 - logistic))
    gate_grad = (hidden_grad * up_pre * slope).astype(BF16)
    up_grad = (hidden_grad * gate_pre * logistic).astype(BF16)
    late = lambda a, b: jnp.einsum("rd,rf->df", a, b, preferred_element_type=F32)
    gate_part = late(rows_x, gate_grad[:, half:]).astype(BF16)
    up_part = late(rows_x, up_grad[:, half:]).astype(BF16)
    out_part = late(hidden[:, half:], rows_d).astype(BF16)
    gate_grad, up_grad, gate_part, up_part, out_part = tie(
        gate_grad, up_grad, gate_part, up_part, out_part
    )
    both = jnp.concatenate([gate_grad, up_grad], axis=1)
    q_part = jnp.einsum("rf,df->rd", both, w_in, preferred_element_type=F32).astype(BF16)
    y_up, y_down, *y_1 = tie(*scatter_far(y_part, *y_1), *y_1)
    y_2 = far_z(y_up, y_down)
    q_up, q_down, *y_1 = tie(*scatter_in(q_part), *y_1)
    q_1 = far_z(q_up, q_down)
    y_rows = scatter_out(y_part, *y_1, *y_2)
    back_out = to_slots(y_rows)
    q_up, q_down, back_out, *q_1 = tie(*scatter_far(q_part, *q_1), back_out, *q_1)
    q_2 = far_z(q_up, q_down)
    q_rows = scatter_out(q_part, *q_1, *q_2)

    gate_got = lax.ppermute(gate_part, "core", SWAP)
    up_got = lax.ppermute(up_part, "core", SWAP)
    out_got = lax.ppermute(out_part, "core", SWAP)
    grad_gate = add(late(rows_x, gate_grad[:, :half]), gate_got)
    grad_up = add(late(rows_x, up_grad[:, :half]), up_got)
    grad_down = add(late(hidden[:, :half], rows_d), out_got)

    back_in = to_slots(q_rows)
    mixed = jnp.einsum(
        "tgc,gcd->td", twice_w, back_out.astype(F32), precision=lax.Precision.HIGHEST
    ).astype(BF16)
    grad_tokens = jnp.einsum(
        "tgc,gcd->td", twice_b, back_in, preferred_element_type=F32
    ).astype(BF16)
    return (mixed, grad_tokens, grad_gate[None], grad_up[None], grad_down[None])


def solution(mesh):
    fine = Mesh(mesh.devices.reshape(2, 4, 2, 4, 2), PAIR + REST)
    rows = P(PAIR + REST, None)
    wide = P(PAIR, None, REST)
    tall = P(PAIR, REST, None)
    return jax.shard_map(
        local,
        mesh=fine,
        in_specs=(rows, rows, rows, rows, wide, wide, tall),
        out_specs=(rows, rows, wide, wide, tall),
        check_vma=False,
    )
```

```python
import jax
import jax.numpy as jnp
from jax import lax
from jax.sharding import Mesh, PartitionSpec as P

CAP = 4
LINE = 4 * CAP
PAIR = ("xl", "y")
REST = ("xh", "z", "core")
PLANE = ("xl", "xh", "y")
SWAP = [(0, 1), (1, 0)]
F32 = jnp.float32
BF16 = jnp.bfloat16
def z_by(step):
    return [(i, (i + step) % 4) for i in range(4)]


def tie(*values):
    return lax.optimization_barrier(values)


def add(*terms):
    return sum(t.astype(F32) for t in terms).astype(BF16)


def near_z(rows):
    return lax.ppermute(rows, "z", z_by(1)), lax.ppermute(rows, "z", z_by(3))


def halves(below, above):
    cut = below.shape[0] // 2
    return below[:cut], above[cut:]


def far_z(low, high):
    return lax.ppermute(low, "z", z_by(1)), lax.ppermute(high, "z", z_by(3))


def across(rows):
    return lax.ppermute(rows, "xh", SWAP)


def near_x(below, above):
    return across(jnp.concatenate([below[:LINE], above[:LINE]], axis=0))


def all_rows(plane, below, above, low, high, near, far):
    return jnp.concatenate(
        [plane, above, near[LINE:], low, high, far, below, near[:LINE]], axis=0
    )


def scatter_in(parts):
    cut = parts.shape[0] // 8
    return parts[3 * cut : 5 * cut], parts[5 * cut : 7 * cut]


def scatter_far(parts, up_1, down_1):
    cut = parts.shape[0] // 8
    return add(parts[2 * cut : 3 * cut], up_1[cut:]), add(parts[7 * cut :], down_1[:cut])


def scatter_out(parts, up_1, down_1, up_2, down_2):
    cut = parts.shape[0] // 8
    top = add(parts[:cut], down_1[cut:], up_2)
    low = add(parts[cut : 2 * cut], up_1[:cut], down_2)
    return jnp.concatenate([top, low], axis=0)


def relative(blocks):
    xl, xh = lax.axis_index("xl"), lax.axis_index("xh")
    same = jnp.where(xl == 0, blocks[:2], blocks[2:])
    other = jnp.where(xl == 0, blocks[2:], blocks[:2])
    own = jnp.where(xh == 0, same[0], same[1])
    far = jnp.where(xh == 0, same[1], same[0])
    return jnp.concatenate([own, other.reshape(2 * LINE, -1), far], axis=0)


def absolute(rows):
    xl, xh = lax.axis_index("xl"), lax.axis_index("xh")
    own, far = rows[:LINE], rows[3 * LINE :]
    other = rows[LINE : 3 * LINE]
    same = jnp.concatenate([jnp.where(xh == 0, own, far), jnp.where(xh == 0, far, own)], axis=0)
    first, second = jnp.where(xl == 0, same, other), jnp.where(xl == 0, other, same)
    return jnp.concatenate([first, second], axis=0)


def to_plane(slots):
    width = slots.shape[-1]
    twice = jnp.broadcast_to(slots.reshape(2, 1, 4, CAP, width), (2, 2, 4, CAP, width))
    return twice.reshape(16, CAP, width)


def move_plane(twice):
    moved = lax.all_to_all(twice, PLANE, split_axis=0, concat_axis=0, tiled=True)
    return relative(moved.reshape(4, LINE, -1))


def to_slots(rows):
    width = rows.shape[1]
    sent = absolute(rows).reshape(16, CAP, width)
    back = lax.all_to_all(sent, PLANE, split_axis=0, concat_axis=0, tiled=True)
    return back


def local(tokens, route, gates, cotangent, w_gate, w_up, w_down):
    model_width = tokens.shape[1]
    half = w_down.shape[1]
    matches = route[:, :, None] == jnp.arange(8, dtype=jnp.int32)
    member = jnp.any(matches, axis=1)
    weight = jnp.sum(jnp.where(matches, gates[:, :, None], 0.0), axis=1)
    rows = jnp.arange(route.shape[0])
    earlier = (rows[None, :] < rows[:, None]).astype(BF16)
    places = jnp.dot(earlier, member.astype(BF16), preferred_element_type=F32)
    picked = member[:, :, None] & (places[:, :, None] == jnp.arange(CAP, dtype=F32))
    picked_b = picked.astype(BF16).reshape(-1, 8 * CAP)
    picked_w = jnp.where(picked, weight[:, :, None], 0.0)
    pair = lambda a: jnp.broadcast_to(a.reshape(-1, 2, 1, 4, CAP), (a.shape[0], 2, 2, 4, CAP))
    twice_b = pair(picked.astype(BF16)).reshape(-1, 16, CAP)
    twice_w = pair(picked_w).reshape(-1, 16, CAP)
    picked_w = picked_w.reshape(-1, 8 * CAP)
    slot_gate = jnp.sum(picked_w, axis=0)
    gate_other = lax.ppermute(w_gate[0], "core", SWAP)
    up_other = lax.ppermute(w_up[0], "core", SWAP)
    down_other = lax.ppermute(w_down[0], "core", SWAP)

    d_rows = jnp.einsum("ts,td->sd", picked_b, cotangent, preferred_element_type=F32)
    d_slots = (d_rows * slot_gate[:, None]).astype(BF16)
    x_twice = jnp.einsum("tgc,td->gcd", twice_b, tokens, preferred_element_type=F32)
    plane_x = move_plane(x_twice.astype(BF16))
    x_near = near_z(plane_x[: 3 * LINE])
    d_twice, plane_x = tie(to_plane(d_slots), plane_x)
    plane_d = move_plane(d_twice)
    x_far = far_z(*tie(*halves(*x_near)))
    x_side = near_x(*x_near)
    d_ring, *x_near = tie(plane_d[: 3 * LINE], *x_near)
    d_near = near_z(d_ring)
    x_last = across(x_far[0][:LINE])
    tied = tie(w_gate[0], gate_other, w_up[0], up_other, w_down[0], down_other, *x_far)
    parts, x_far = tied[:6], tied[6:]
    w_in = jnp.concatenate(parts[:4], axis=1)
    w_out = jnp.concatenate(parts[4:], axis=0)
    w_in, w_out = tie(w_in, w_out)
    rows_x = all_rows(plane_x, *x_near, *x_far, x_side, x_last)

    pre = jnp.dot(rows_x, w_in, preferred_element_type=F32)
    gate_pre, up_pre = pre[:, : 2 * half], pre[:, 2 * half :]
    logistic = jax.nn.sigmoid(gate_pre)
    hidden = (gate_pre * logistic * up_pre).astype(BF16)
    hidden, gate_pre, up_pre = tie(hidden, gate_pre, up_pre)
    d_low, d_high = tie(*halves(*d_near))
    d_far = far_z(d_low, d_high)
    d_side = near_x(*d_near)
    y_part = jnp.dot(hidden, w_out, preferred_element_type=F32).astype(BF16)
    d_last = across(d_far[0][:LINE])
    y_up, y_down, *d_far = tie(*scatter_in(y_part), *d_far)
    y_1 = far_z(y_up, y_down)
    rows_d = all_rows(plane_d, *d_near, *d_far, d_side, d_last)

    hidden_grad = jnp.einsum("rd,fd->rf", rows_d, w_out, preferred_element_type=F32)
    logistic = jax.nn.sigmoid(gate_pre)
    slope = logistic * (1.0 + gate_pre * (1.0 - logistic))
    gate_grad = (hidden_grad * up_pre * slope).astype(BF16)
    up_grad = (hidden_grad * gate_pre * logistic).astype(BF16)
    late = lambda a, b: jnp.einsum("rd,rf->df", a, b, preferred_element_type=F32)
    gate_part = late(rows_x, gate_grad[:, half:]).astype(BF16)
    up_part = late(rows_x, up_grad[:, half:]).astype(BF16)
    out_part = late(hidden[:, half:], rows_d).astype(BF16)
    gate_grad, up_grad, gate_part, up_part, out_part = tie(
        gate_grad, up_grad, gate_part, up_part, out_part
    )
    both = jnp.concatenate([gate_grad, up_grad], axis=1)
    q_part = jnp.einsum("rf,df->rd", both, w_in, preferred_element_type=F32).astype(BF16)
    y_up, y_down, *y_1 = tie(*scatter_far(y_part, *y_1), *y_1)
    y_2 = far_z(y_up, y_down)
    q_up, q_down, *y_1 = tie(*scatter_in(q_part), *y_1)
    q_1 = far_z(q_up, q_down)
    y_rows = scatter_out(y_part, *y_1, *y_2)
    back_out = to_slots(y_rows)
    q_up, q_down, back_out, *q_1 = tie(*scatter_far(q_part, *q_1), back_out, *q_1)
    q_2 = far_z(q_up, q_down)
    q_rows = scatter_out(q_part, *q_1, *q_2)

    gate_got = lax.ppermute(gate_part, "core", SWAP)
    up_got = lax.ppermute(up_part, "core", SWAP)
    out_got = lax.ppermute(out_part, "core", SWAP)
    grad_gate = add(late(rows_x, gate_grad[:, :half]), gate_got)
    grad_up = add(late(rows_x, up_grad[:, :half]), up_got)
    grad_down = add(late(hidden[:, :half], rows_d), out_got)

    back_in = to_slots(q_rows)
    mixed = jnp.einsum(
        "tgc,gcd->td", twice_w, back_out.astype(F32), precision=lax.Precision.HIGHEST
    ).astype(BF16)
    grad_tokens = jnp.einsum(
        "tgc,gcd->td", twice_b, back_in, preferred_element_type=F32
    ).astype(BF16)
    return (mixed, grad_tokens, grad_gate[None], grad_up[None], grad_down[None])


def solution(mesh):
    fine = Mesh(mesh.devices.reshape(2, 4, 2, 4, 2), PAIR + REST)
    rows = P(PAIR + REST, None)
    wide = P(PAIR, None, REST)
    tall = P(PAIR, REST, None)
    return jax.shard_map(
        local,
        mesh=fine,
        in_specs=(rows, rows, rows, rows, wide, wide, tall),
        out_specs=(rows, rows, wide, wide, tall),
        check_vma=False,
    )
```
